32 devices in a mesh: survey: 2 (over x), chan: 16 (over z, y, core).
Axes of the slice: x: 2, y: 2, z: 4, core: 2. Of those that a mesh axis runs over, the one named last changes fastest.
Arguments:
- das_window: float32 [8192, 8192], P(('survey', 'chan')), parts along dimension 0, may hold values from -6 to 6
- fan_bound: int32 [4096], replicated, may hold values from -1 to 2048, as said below
- tap_offset: int32 [8, 32], replicated, may hold values from -31 to 31, as said below
- tap_weight: float32 [8, 32], replicated, may hold values from -1 to 1
Outputs:
- filtered: float32 [8192, 8192], P(('survey', 'chan')), parts along dimension 0
- energy: float32 [8192, 8, 128], P(('survey', 'chan')), parts along dimension 0
The draws below stay inside these ranges and needn't reach their ends.
There are 2 independent parts, one for each index of `survey`. The reference program is written for one: setup_inputs(seed, part) draws one part's arguments, and reference() takes and returns one part's arrays. A program takes and returns all parts, laid end to end along the dimension named above; an argument that names none is the same for every part. Nothing has to cross between parts.
Inputs may be any that keep to these rules, and one draw needn't show every extreme that they name: `fan_bound`: entry f bounds the magnitude of the signed channel wavenumber bin passed at the time frequency bins +f and -f; -1 passes none. `tap_offset`: the channel offset of a tap relative to the output channel.
All inputs are finite; a program needn't handle non-finite values.
Results may differ from the reference program's by a relative error of at most 0.0027.
Values may be sent and summed in bfloat16 or wider, within the bound.
No kernel may reach another device: no remote copies, remote signals or barrier semaphores. Data moves between devices by JAX's collectives and lax.ppermute only.
A program may use at most 256 MiB of HBM per device.

```python
import jax
import jax.numpy as jnp
from jax import lax

S = 8192
HALO = 31
TEMPLATES = 8
TAPS = 32
WIN = 64
C = 4096


def draw_fan_bound(key, part):
    freq_index = jnp.arange(S // 2, dtype=jnp.int32)
    low_cut = jax.random.randint(jax.random.fold_in(key, 1), (), 1, max(2, S // 8))
    slope_rate = jax.random.randint(jax.random.fold_in(key, 2), (), 3, 7)
    jitter_span = max(1, C // 256)
    jitter = jax.random.randint(jax.random.fold_in(key, 3), (S // 2,), -jitter_span, jitter_span + 1)
    linear = (freq_index - low_cut) * slope_rate * C // (2 * S)
    bounded = jnp.clip(linear + jitter, -1, C // 2)
    bounded = jnp.where(freq_index < low_cut, -1, bounded)
    return bounded.astype(jnp.int32)


def draw_tap_offset(key, part):
    raw_offsets = jax.random.randint(jax.random.fold_in(key, 1), (TEMPLATES * TAPS,), -HALO, HALO + 1)
    ordering = jax.random.permutation(jax.random.fold_in(key, 2), TEMPLATES * TAPS)
    raw_offsets = raw_offsets.at[ordering[0]].set(-HALO)
    raw_offsets = raw_offsets.at[ordering[1]].set(HALO)
    return raw_offsets.reshape(TEMPLATES, TAPS).astype(jnp.int32)


def block_scale(key, shape, cuts, smallest, largest):
    loudness = 1.0
    for position, blocks in cuts:
        draws = jax.random.uniform(jax.random.fold_in(jax.random.fold_in(key, 6), position), (blocks,), jnp.float32, smallest / len(cuts), largest / len(cuts))
        loudness = loudness * jnp.repeat(jnp.exp(draws), shape[position] // blocks).reshape((-1,) + (1,) * (len(shape) - 1 - position))
    return loudness


def noise(stream_key, dims, width, most, split=(), kind=jnp.bfloat16):
    values = jax.random.normal(stream_key, dims, jnp.float32) * width
    if len(split) > 0:
        values = block_scale(stream_key, dims, split, -0.22, 0.18) * values
    return jnp.clip(values, min=-most, max=most).astype(kind)


def setup_inputs(seed: int = 0, part: int = 0) -> dict:
    keys = jax.random.split(jax.random.key(seed), 5)
    part_keys = jax.random.split(jax.random.fold_in(keys[4], part), 5)
    return {
        "das_window": noise(part_keys[0], (C, S), 1.0, 6.0, ((0, 16),), jnp.float32),
        "fan_bound": draw_fan_bound(jax.random.fold_in(keys[4], 71), part),
        "tap_offset": draw_tap_offset(jax.random.fold_in(keys[4], 71), part),
        "tap_weight": noise(keys[3], (TEMPLATES, TAPS), TAPS ** -0.5, 1.0, (), jnp.float32),
    }


def reference(das_window, fan_bound, tap_offset, tap_weight):
    spectrum = jnp.fft.fft2(das_window)
    chan_index = jnp.arange(C, dtype=jnp.int32)
    chan_signed = jnp.where(chan_index < C // 2, chan_index, chan_index - C)
    time_index = jnp.arange(S, dtype=jnp.int32)
    time_signed = jnp.where(time_index < S // 2, time_index, time_index - S)
    extended = jnp.concatenate([fan_bound, jnp.full((1,), -1, jnp.int32)])
    limits = jnp.take(extended, jnp.abs(time_signed).astype(jnp.int32))
    passing = jnp.abs(chan_signed)[:, None] <= limits[None, :]
    filtered = jnp.fft.ifft2(jnp.where(passing, spectrum, 0.0)).real.astype(jnp.float32)
    rounded = filtered.astype(jnp.bfloat16)
    low_field = lax.optimization_barrier(rounded).astype(jnp.float32)
    offsets_grid = jnp.arange(2 * HALO + 1, dtype=jnp.int32) - HALO
    matches = (tap_offset[:, :, None] == offsets_grid[None, None, :]).astype(jnp.float32)
    kernel_low = jnp.sum(tap_weight[:, :, None] * matches, axis=1).astype(jnp.bfloat16)
    kernel_wide = lax.optimization_barrier(kernel_low).astype(jnp.float32)
    padded = jnp.pad(low_field, ((HALO, HALO), (0, 0)))

    def one_template(weights):
        def add_offset(offset, running):
            return running + weights[offset] * lax.dynamic_slice_in_dim(padded, offset, C, 0)

        detection = lax.fori_loop(0, 2 * HALO + 1, add_offset, jnp.zeros((C, S), jnp.float32))
        return jnp.mean((detection * detection).reshape(C, S // WIN, WIN), axis=2)

    energy = lax.map(one_template, kernel_wide)
    return filtered, jnp.transpose(energy, (1, 0, 2))
```

```python
import functools
import math

import jax
import jax.numpy as jnp
import ml_dtypes
import numpy as np
from jax import lax
from jax.experimental import pallas as pl
from jax.experimental.pallas import tpu as pltpu
from jax.sharding import PartitionSpec as P

HALO = 31
WIN = 64
RADIX = 32
LANES = 256
SLOTS = RADIX // 2
COLS = 2 * LANES
BF = jnp.bfloat16
F32 = jnp.float32


def split_table(table):
    high = table.astype(ml_dtypes.bfloat16)
    low = (table - high.astype(np.float64)).astype(ml_dtypes.bfloat16)
    return np.stack([high, low])


def full_table():
    index = np.arange(LANES)
    angle = 2.0 * np.pi * ((index[:, None] * index[None, :]) % LANES) / LANES
    cos, sin = np.cos(angle), np.sin(angle)
    return np.block([[cos, -sin], [sin, cos]])


def paired_table():
    half = LANES // 2
    sample = np.arange(LANES)[:, None]
    even = 2 * np.arange(half)[None, :]
    odd = 1 + 2 * np.arange(half)[None, ::-1]
    step = 2.0 * np.pi / (2 * LANES)
    even_angle, odd_angle = (sample * even) * step, (sample * odd) * step
    table = np.zeros((COLS, COLS))
    table[:LANES, :half] = np.cos(even_angle)
    table[:LANES, LANES : LANES + half] = -np.sin(even_angle)
    table[:LANES, LANES] = np.cos(np.pi * sample[:, 0])
    table[LANES:, half:LANES] = np.cos(odd_angle)
    table[LANES:, LANES + half :] = -np.sin(odd_angle)
    return table


def real_dft(values):
    count = len(values)
    if count == 2:
        return [(values[0] + values[1], None), (values[0] - values[1], None)]
    even, odd = real_dft(values[0::2]), real_dft(values[1::2])
    quarter = count // 4
    out = [None] * (count // 2 + 1)
    out[0] = (even[0][0] + odd[0][0], None)
    out[count // 2] = (even[0][0] - odd[0][0], None)
    out[quarter] = (even[quarter][0], -odd[quarter][0])
    for k in range(1, quarter):
        cos, sin = math.cos(2 * math.pi * k / count), math.sin(2 * math.pi * k / count)
        (er, ei), (dr, di) = even[k], odd[k]
        tr, ti = dr * cos + di * sin, di * cos - dr * sin
        out[k] = (er + tr, ei + ti)
        out[count // 2 - k] = (er - tr, ti - ei)
    return out


def real_idft(bins):
    count = 2 * (len(bins) - 1)
    if count == 2:
        return [bins[0][0] + bins[1][0], bins[0][0] - bins[1][0]]
    quarter = count // 4
    first, last = bins[0][0], bins[count // 2][0]
    even, odd = [(first + last, None)], [(first - last, None)]
    for k in range(1, quarter):
        cos, sin = math.cos(2 * math.pi * k / count), math.sin(2 * math.pi * k / count)
        (ar, ai), (br, bi) = bins[k], bins[count // 2 - k]
        even.append((ar + br, ai - bi))
        dr, di = ar - br, ai + bi
        odd.append((dr * cos - di * sin, dr * sin + di * cos))
    mr, mi = bins[quarter]
    even.append((2.0 * mr, None))
    odd.append((-2.0 * mi, None))
    out = [None] * count
    out[0::2] = real_idft(even)
    out[1::2] = real_idft(odd)
    return out


def parts_of(value):
    high = value.astype(BF)
    return high, (value - high.astype(F32)).astype(BF)


def dot(left, right):
    return jnp.dot(left, right, preferred_element_type=F32)


def dot_t(left, right):
    return lax.dot_general(left, right, (((1,), (1,)), ((), ())), preferred_element_type=F32)


def forward_kernel(x_ref, tw_ref, full_ref, pair_ref, out_ref, y_ref):
    rows = x_ref.shape[0]
    pieces = out_ref.shape[1]
    width = COLS // pieces

    def group(i, carry):
        span = pl.ds(pl.multiple_of(i * 8, 8), 8)
        for half in range(2):
            at = slice(128 * half, 128 * half + 128)
            to = slice(LANES + 128 * half, LANES + 128 * half + 128)
            values = [
                x_ref[span, LANES * a + 128 * half : LANES * a + 128 * half + 128]
                for a in range(RADIX)
            ]
            bins = real_dft(values)
            y_ref[0, span, at] = bins[0][0]
            y_ref[0, span, to] = bins[SLOTS][0]
            for k in range(1, SLOTS):
                cos, sin = tw_ref[k : k + 1, at], tw_ref[SLOTS + k : SLOTS + k + 1, at]
                re, im = bins[k]
                y_ref[k, span, at] = re * cos + im * sin
                y_ref[k, span, to] = im * cos - re * sin
        return carry

    lax.fori_loop(0, rows // 8, group, 0)

    def put(first, slots, value):
        value = value.astype(BF)
        for piece in range(pieces):
            part = value[:, width * piece : width * (piece + 1)]
            out_ref[pl.ds(first, slots), piece] = part.reshape(slots, rows, width)

    def product(first, slots, table):
        high, low = parts_of(y_ref[pl.ds(first, slots)].reshape(slots * rows, COLS))
        put(first, slots, dot(high, table[0]) + dot(low, table[0]) + dot(high, table[1]))

    product(0, 1, pair_ref)

    def batch(g, carry):
        product(1 + 5 * g, 5, full_ref)
        return carry

    lax.fori_loop(0, 3, batch, 0)


def forward(x, tw, full, pair, pieces):
    rows, samples = x.shape
    tile = 64
    return pl.pallas_call(
        forward_kernel,
        grid=(rows // tile,),
        in_specs=[
            pl.BlockSpec((tile, samples), lambda i: (i, 0)),
            pl.BlockSpec(tw.shape, lambda i: (0, 0)),
            pl.BlockSpec(full.shape, lambda i: (0, 0, 0)),
            pl.BlockSpec(pair.shape, lambda i: (0, 0, 0)),
        ],
        out_specs=pl.BlockSpec((SLOTS, pieces, tile, COLS // pieces), lambda i: (0, 0, i, 0)),
        out_shape=jax.ShapeDtypeStruct((SLOTS, pieces, rows, COLS // pieces), BF),
        scratch_shapes=[pltpu.VMEM((SLOTS, tile, COLS), F32)],
        compiler_params=pltpu.CompilerParams(vmem_limit_bytes=56 << 20),
        name="time_forward",
    )(x, tw, full, pair)


def channel_kernel(z_ref, bound_ref, tab_ref, full_ref, pair_ref, pair_t_ref, out_ref, y_ref, tw_ref):
    peers = z_ref.shape[0]
    slots = peers // 2
    scale = 1.0 / (peers * LANES)

    @pl.when(pl.program_id(0) == 0)
    def _():
        for k in range(1, slots):
            tw_ref[k] = jnp.broadcast_to(tab_ref[:, k : k + 1], (LANES, 128))
            tw_ref[slots + k] = jnp.broadcast_to(tab_ref[:, 64 + k : 65 + k], (LANES, 128))

    def spans(i):
        low = pl.multiple_of(i * 16, 16)
        return pl.ds(low, 16), pl.ds(pl.multiple_of(LANES + low, 16), 16)

    def before(i, carry):
        span, span_im = spans(i)
        bins = real_dft([z_ref[d, span, :].astype(F32) for d in range(peers)])
        y_ref[span, 0:128] = bins[0][0]
        y_ref[span_im, 0:128] = bins[slots][0]
        for k in range(1, slots):
            cos, sin = tw_ref[k, span, :], tw_ref[slots + k, span, :]
            re, im = bins[k]
            y_ref[span, 128 * k : 128 * k + 128] = re * cos + im * sin
            y_ref[span_im, 128 * k : 128 * k + 128] = re * sin - im * cos
        return carry

    lax.fori_loop(0, LANES // 16, before, 0)
    bound = bound_ref[...]

    def product(table, value):
        high, low = parts_of(value)
        return dot(table[0], high) + dot(table[0], low) + dot(table[1], high)

    row = lax.broadcasted_iota(jnp.int32, (COLS, 128), 0)
    inner = row & (LANES - 1)
    reach = jnp.where(inner < LANES // 2, peers * inner, peers // 2 + peers * (LANES - 1 - inner))
    reach = jnp.where(row == LANES, peers * (LANES // 2), reach)
    gain = jnp.where((row == 0) | (row == LANES), scale, 2.0 * scale)
    spec = product(pair_t_ref, y_ref[:, 0:128])
    spec = jnp.where(reach <= bound, spec * gain, 0.0)
    y_ref[:, 0:128] = product(pair_ref, spec)

    def filtered(first, width):
        at = pl.ds(pl.multiple_of(first * 128, 128), width)
        spec = product(full_ref, y_ref[:, at])
        inner = lax.broadcasted_iota(jnp.int32, (LANES, width), 0)
        lane = lax.broadcasted_iota(jnp.int32, (LANES, width), 1)
        k1 = first + lane // 128
        reach = jnp.where(inner < LANES // 2, k1 + peers * inner, peers * (LANES - inner) - k1)
        wide = bound if width == 128 else jnp.concatenate([bound] * (width // 128), axis=1)
        keep = reach <= wide
        spec = jnp.concatenate(
            [jnp.where(keep, spec[:LANES], 0.0), jnp.where(keep, -spec[LANES:], 0.0)], axis=0
        )
        y_ref[:, at] = product(full_ref, spec)

    def pairs(j, carry):
        filtered(1 + 2 * j, 256)
        return carry

    lax.fori_loop(0, slots // 2 - 1, pairs, 0)
    filtered(slots - 1, 128)

    def after(i, carry):
        span, span_im = spans(i)
        bins = [(y_ref[span, 0:128], None)]
        for k in range(1, slots):
            cos, sin = tw_ref[k, span, :] * scale, tw_ref[slots + k, span, :] * scale
            re, im = y_ref[span, 128 * k : 128 * k + 128], y_ref[span_im, 128 * k : 128 * k + 128]
            bins.append((re * cos - im * sin, re * sin + im * cos))
        bins.append((y_ref[span_im, 0:128], None))
        for d, value in enumerate(real_idft(bins)):
            out_ref[d, span, :] = value.astype(BF)
        return carry

    lax.fori_loop(0, LANES // 16, after, 0)


def channel_filter(z, bound, tab, full, pair, pair_t):
    peers, rows, width = z.shape
    const3 = lambda i: (0, 0, 0)
    return pl.pallas_call(
        channel_kernel,
        grid=(width // 128,),
        in_specs=[
            pl.BlockSpec((peers, rows, 128), lambda i: (0, 0, i)),
            pl.BlockSpec((1, 128), lambda i: (0, i)),
            pl.BlockSpec(tab.shape, lambda i: (0, 0)),
            pl.BlockSpec(full.shape, const3),
            pl.BlockSpec(pair.shape, const3),
            pl.BlockSpec(pair_t.shape, const3),
        ],
        out_specs=pl.BlockSpec((peers, rows, 128), lambda i: (0, 0, i)),
        out_shape=jax.ShapeDtypeStruct(z.shape, BF),
        scratch_shapes=[
            pltpu.VMEM((COLS, peers // 2 * 128), F32),
            pltpu.VMEM((peers, LANES, 128), F32),
        ],
        compiler_params=pltpu.CompilerParams(vmem_limit_bytes=56 << 20),
        name="channel_filter",
    )(z, bound, tab, full, pair, pair_t)


def inverse_kernel(z_ref, tw_ref, full_ref, pair_ref, out_ref, v_ref):
    pieces, rows = z_ref.shape[1], z_ref.shape[2]
    width = COLS // pieces
    scale = 1.0 / (RADIX * LANES)

    def product(first, slots, table, gain):
        total = None
        for piece in range(pieces):
            at = slice(width * piece, width * (piece + 1))
            value = z_ref[pl.ds(first, slots), piece].reshape(slots * rows, width)
            if gain is not None:
                value = value * gain[:, at]
            for level in range(2):
                term = dot_t(value, table[level, :, at])
                total = term if total is None else total + term
        v_ref[pl.ds(first, slots)] = total.reshape(slots, rows, COLS)

    lane = lax.broadcasted_iota(jnp.int32, (1, COLS), 1)
    gain = jnp.where((lane == 0) | (lane == LANES), scale, 2.0 * scale).astype(BF)
    product(0, 1, pair_ref, gain)

    def batch(g, carry):
        product(1 + 5 * g, 5, full_ref, None)
        return carry

    lax.fori_loop(0, 3, batch, 0)

    def group(i, carry):
        span = pl.ds(pl.multiple_of(i * 8, 8), 8)
        for half in range(2):
            at = slice(128 * half, 128 * half + 128)
            to = slice(LANES + 128 * half, LANES + 128 * half + 128)
            bins = [(v_ref[0, span, at], None)]
            for k in range(1, SLOTS):
                cos = tw_ref[k : k + 1, at] * scale
                sin = tw_ref[SLOTS + k : SLOTS + k + 1, at] * scale
                re, im = v_ref[k, span, at], v_ref[k, span, to]
                bins.append((re * cos - im * sin, re * sin + im * cos))
            bins.append((v_ref[0, span, to], None))
            for a, value in enumerate(real_idft(bins)):
                out_ref[span, LANES * a + 128 * half : LANES * a + 128 * half + 128] = value
        return carry

    lax.fori_loop(0, rows // 8, group, 0)


def inverse(z, tw, full, pair):
    slots, pieces, rows, width = z.shape
    samples = RADIX * LANES
    tile = 64
    return pl.pallas_call(
        inverse_kernel,
        grid=(rows // tile,),
        in_specs=[
            pl.BlockSpec((slots, pieces, tile, width), lambda i: (0, 0, i, 0)),
            pl.BlockSpec(tw.shape, lambda i: (0, 0)),
            pl.BlockSpec(full.shape, lambda i: (0, 0, 0)),
            pl.BlockSpec(pair.shape, lambda i: (0, 0, 0)),
        ],
        out_specs=pl.BlockSpec((tile, samples), lambda i: (i, 0)),
        out_shape=jax.ShapeDtypeStruct((rows, samples), F32),
        scratch_shapes=[pltpu.VMEM((SLOTS, tile, COLS), F32)],
        compiler_params=pltpu.CompilerParams(vmem_limit_bytes=56 << 20),
        name="time_inverse",
    )(z, tw, full, pair)


def detect_kernel(before_ref, mid_ref, after_ref, stack_ref, out_ref, sums_ref):
    rows, span = mid_ref.shape
    step = pl.program_id(0)
    block = 512
    tiles = rows // 32
    for b in range(span // block):
        at = slice(block * b, block * (b + 1))
        low = jnp.concatenate(
            [
                before_ref[:, at].astype(F32),
                mid_ref[:, at],
                after_ref[:, at].astype(F32),
                jnp.zeros((64, block), F32),
            ],
            axis=0,
        )
        turned = low.T.astype(BF)
        for j in range(tiles):
            base = j // 4 * 128
            shift = 96 - 32 * (j % 4)
            detection = dot(turned[:, base : base + 256], stack_ref[shift : shift + 256, :])
            squared = (detection * detection).reshape(block // WIN, WIN, 256)
            first = pl.multiple_of(step * (span // WIN) + b * (block // WIN), 8)
            sums_ref[pl.ds(first, 8), 256 * j : 256 * j + 256] = jnp.sum(squared, axis=1)

    @pl.when(step == pl.num_programs(0) - 1)
    def _():
        out_ref[...] = sums_ref[...].T * (1.0 / WIN)


def detect(before, filtered, after, stack, templates):
    rows, samples = filtered.shape
    span = 1024
    windows = samples // WIN
    return pl.pallas_call(
        detect_kernel,
        grid=(samples // span,),
        in_specs=[
            pl.BlockSpec((32, span), lambda i: (0, i)),
            pl.BlockSpec((rows, span), lambda i: (0, i)),
            pl.BlockSpec((32, span), lambda i: (0, i)),
            pl.BlockSpec(stack.shape, lambda i: (0, 0)),
        ],
        out_specs=pl.BlockSpec((rows * templates, windows), lambda i: (0, 0)),
        out_shape=jax.ShapeDtypeStruct((rows * templates, windows), F32),
        scratch_shapes=[pltpu.VMEM((windows, rows * templates), F32)],
        compiler_params=pltpu.CompilerParams(vmem_limit_bytes=56 << 20),
        name="detect",
    )(before, filtered, after, stack)


def bin_bounds(fan_bound):
    by_bin = fan_bound.reshape(LANES // 2, RADIX).T
    falling = by_bin[:, ::-1]
    mirror = jnp.concatenate([falling[SLOTS : SLOTS + 1], falling[:SLOTS:-1]], axis=0)
    real_part = jnp.concatenate([by_bin[:SLOTS], mirror], axis=1)
    bounds = jnp.concatenate([real_part, real_part], axis=1)
    return bounds.at[0, LANES].set(-1)


def stacking(tap_offset, tap_weight):
    span = 2 * HALO + 1
    templates = tap_offset.shape[0]
    offsets_grid = jnp.arange(span, dtype=jnp.int32) - HALO
    matches = (tap_offset[:, :, None] == offsets_grid[None, None, :]).astype(F32)
    kernel_low = jnp.sum(tap_weight[:, :, None] * matches, axis=1).astype(BF)
    period = 257
    line = jnp.pad(kernel_low, ((0, 0), (1, period - 1 - span)))
    band = jnp.tile(line, (1, 32))[:, : 32 * 256].reshape(templates, 32, 256)
    band = jnp.transpose(band, (2, 1, 0)).reshape(256, 32 * templates)
    return jnp.pad(band, ((96, 0), (0, 0)))


def per_device(das_window, fan_bound, tap_offset, tap_weight):
    rows, samples = das_window.shape
    peers = lax.axis_size("chan")
    pieces = peers // SLOTS
    templates = tap_offset.shape[0]
    me = lax.axis_index("chan")
    full = jnp.asarray(split_table(full_table()))
    pair_np = split_table(paired_table())
    pair = jnp.asarray(pair_np)
    pair_t = jnp.asarray(np.ascontiguousarray(np.swapaxes(pair_np, 1, 2)))
    order = np.arange(SLOTS)[:, None] * np.arange(LANES)[None, :]
    angle = 2.0 * np.pi * order / samples
    tw = jnp.asarray(np.concatenate([np.cos(angle), np.sin(angle)]).astype(np.float32))
    tab_np = np.zeros((LANES, 128), np.float32)
    order = np.arange(LANES)[:, None] * np.arange(peers // 2)[None, :]
    angle = 2.0 * np.pi * order / (peers * LANES)
    tab_np[:, : peers // 2] = np.cos(angle)
    tab_np[:, 64 : 64 + peers // 2] = np.sin(angle)
    tab = jnp.asarray(tab_np)

    width = COLS // pieces
    bounds = bin_bounds(fan_bound).reshape(peers, width)
    bound = lax.dynamic_slice_in_dim(bounds, me, 1, 0)
    stack = stacking(tap_offset, tap_weight)

    spectrum = forward(das_window, tw, full, pair, pieces)
    sent = spectrum.reshape(peers, rows, width)
    by_freq = lax.all_to_all(sent, "chan", split_axis=0, concat_axis=0, tiled=True)
    wave = channel_filter(by_freq, bound, tab, full, pair, pair_t)
    back = lax.all_to_all(wave, "chan", split_axis=0, concat_axis=0, tiled=True)
    filtered = inverse(back.reshape(SLOTS, pieces, rows, width), tw, full, pair)

    up = [(i, i + 1) for i in range(peers - 1)]
    down = [(i + 1, i) for i in range(peers - 1)]
    before = lax.ppermute(filtered[rows - 32 :].astype(BF), "chan", up)
    after = lax.ppermute(filtered[:32].astype(BF), "chan", down)
    energy = detect(before, filtered, after, stack, templates)
    return filtered, energy.reshape(rows, templates, samples // WIN)


def solution(mesh):
    return jax.shard_map(
        per_device,
        mesh=mesh,
        in_specs=(P(("survey", "chan"), None), P(), P(), P()),
        out_specs=(P(("survey", "chan"), None), P(("survey", "chan"), None, None)),
        check_vma=False,
    )
```

```python
import functools
import math

import jax
import jax.numpy as jnp
import ml_dtypes
import numpy as np
from jax import lax
from jax.experimental import pallas as pl
from jax.experimental.pallas import tpu as pltpu
from jax.sharding import PartitionSpec as P

HALO = 31
WIN = 64
RADIX = 32
LANES = 256
SLOTS = RADIX // 2
COLS = 2 * LANES
BF = jnp.bfloat16
F32 = jnp.float32


def split_table(table):
    high = table.astype(ml_dtypes.bfloat16)
    low = (table - high.astype(np.float64)).astype(ml_dtypes.bfloat16)
    return np.stack([high, low])


def full_table():
    index = np.arange(LANES)
    angle = 2.0 * np.pi * ((index[:, None] * index[None, :]) % LANES) / LANES
    cos, sin = np.cos(angle), np.sin(angle)
    return np.block([[cos, -sin], [sin, cos]])


def paired_table():
    half = LANES // 2
    sample = np.arange(LANES)[:, None]
    even = 2 * np.arange(half)[None, :]
    odd = 1 + 2 * np.arange(half)[None, ::-1]
    step = 2.0 * np.pi / (2 * LANES)
    even_angle, odd_angle = (sample * even) * step, (sample * odd) * step
    table = np.zeros((COLS, COLS))
    table[:LANES, :half] = np.cos(even_angle)
    table[:LANES, LANES : LANES + half] = -np.sin(even_angle)
    table[:LANES, LANES] = np.cos(np.pi * sample[:, 0])
    table[LANES:, half:LANES] = np.cos(odd_angle)
    table[LANES:, LANES + half :] = -np.sin(odd_angle)
    return table


def real_dft(values):
    count = len(values)
    if count == 2:
        return [(values[0] + values[1], None), (values[0] - values[1], None)]
    even, odd = real_dft(values[0::2]), real_dft(values[1::2])
    quarter = count // 4
    out = [None] * (count // 2 + 1)
    out[0] = (even[0][0] + odd[0][0], None)
    out[count // 2] = (even[0][0] - odd[0][0], None)
    out[quarter] = (even[quarter][0], -odd[quarter][0])
    for k in range(1, quarter):
        cos, sin = math.cos(2 * math.pi * k / count), math.sin(2 * math.pi * k / count)
        (er, ei), (dr, di) = even[k], odd[k]
        tr, ti = dr * cos + di * sin, di * cos - dr * sin
        out[k] = (er + tr, ei + ti)
        out[count // 2 - k] = (er - tr, ti - ei)
    return out


def real_idft(bins):
    count = 2 * (len(bins) - 1)
    if count == 2:
        return [bins[0][0] + bins[1][0], bins[0][0] - bins[1][0]]
    quarter = count // 4
    first, last = bins[0][0], bins[count // 2][0]
    even, odd = [(first + last, None)], [(first - last, None)]
    for k in range(1, quarter):
        cos, sin = math.cos(2 * math.pi * k / count), math.sin(2 * math.pi * k / count)
        (ar, ai), (br, bi) = bins[k], bins[count // 2 - k]
        even.append((ar + br, ai - bi))
        dr, di = ar - br, ai + bi
        odd.append((dr * cos - di * sin, dr * sin + di * cos))
    mr, mi = bins[quarter]
    even.append((2.0 * mr, None))
    odd.append((-2.0 * mi, None))
    out = [None] * count
    out[0::2] = real_idft(even)
    out[1::2] = real_idft(odd)
    return out


def parts_of(value):
    high = value.astype(BF)
    return high, (value - high.astype(F32)).astype(BF)


def dot(left, right):
    return jnp.dot(left, right, preferred_element_type=F32)


def dot_t(left, right):
    return lax.dot_general(left, right, (((1,), (1,)), ((), ())), preferred_element_type=F32)


def forward_kernel(x_ref, tw_ref, dest_ref, mask_ref, full_ref, pair_ref, *rest):
    groups = len(rest) - 3
    outs, (full_out, pair_out, y_ref) = rest[:groups], rest[groups:]
    rows = x_ref.shape[0]
    pieces = outs[0].shape[1]

    @pl.when(pl.program_id(0) == 0)
    def _():
        column = lax.broadcasted_iota(jnp.int32, (COLS, COLS), 1)
        moved = (column == dest_ref[...]).astype(F32).astype(BF)
        for level in range(2):
            full_out[level] = dot(full_ref[level], moved).astype(BF)
            pair_out[level] = dot(pair_ref[level], moved).astype(BF)

    def group(i, carry):
        span = pl.ds(pl.multiple_of(i * 8, 8), 8)
        for half in range(2):
            at = slice(128 * half, 128 * half + 128)
            to = slice(LANES + 128 * half, LANES + 128 * half + 128)
            values = [
                x_ref[span, LANES * a + 128 * half : LANES * a + 128 * half + 128]
                for a in range(RADIX)
            ]
            bins = real_dft(values)
            y_ref[0, span, at] = bins[0][0]
            y_ref[0, span, to] = bins[SLOTS][0]
            for k in range(1, SLOTS):
                cos, sin = tw_ref[k : k + 1, at], tw_ref[SLOTS + k : SLOTS + k + 1, at]
                re, im = bins[k]
                y_ref[k, span, at] = re * cos + im * sin
                y_ref[k, span, to] = im * cos - re * sin
        return carry

    lax.fori_loop(0, rows // 8, group, 0)

    def product(first, slots, table):
        high, low = parts_of(y_ref[pl.ds(first, slots)].reshape(slots * rows, COLS))
        value = dot(high, table[0]) + dot(low, table[0]) + dot(high, table[1])
        value = value.reshape(slots, rows, COLS) * mask_ref[pl.ds(first, slots)]
        value = value.astype(BF)
        for g in range(groups):
            for piece in range(pieces):
                lane = 128 * (g * pieces + piece)
                outs[g][pl.ds(first, slots), piece] = value[:, :, lane : lane + 128]

    product(0, 1, pair_out)

    def batch(g, carry):
        product(1 + 5 * g, 5, full_out)
        return carry

    lax.fori_loop(0, 3, batch, 0)


def forward(x, tw, dest, mask, full, pair, pieces):
    rows, samples = x.shape
    tile = 64
    groups = COLS // 128 // pieces
    const2, const3 = lambda i: (0, 0), lambda i: (0, 0, 0)
    chunk = jax.ShapeDtypeStruct((SLOTS, pieces, rows, 128), BF)
    table = jax.ShapeDtypeStruct(full.shape, BF)
    return pl.pallas_call(
        forward_kernel,
        grid=(rows // tile,),
        in_specs=[
            pl.BlockSpec((tile, samples), lambda i: (i, 0)),
            pl.BlockSpec(tw.shape, const2),
            pl.BlockSpec(dest.shape, const2),
            pl.BlockSpec(mask.shape, const3),
            pl.BlockSpec(full.shape, const3),
            pl.BlockSpec(pair.shape, const3),
        ],
        out_specs=[pl.BlockSpec((SLOTS, pieces, tile, 128), lambda i: (0, 0, i, 0))] * groups
        + [pl.BlockSpec(full.shape, const3)] * 2,
        out_shape=[chunk] * groups + [table] * 2,
        scratch_shapes=[pltpu.VMEM((SLOTS, tile, COLS), F32)],
        compiler_params=pltpu.CompilerParams(vmem_limit_bytes=56 << 20),
        name="time_forward",
    )(x, tw, dest, mask, full, pair)


def channel_kernel(z_ref, bound_ref, tab_ref, full_ref, pair_ref, pair_t_ref, out_ref, y_ref, tw_ref):
    peers = z_ref.shape[0]
    slots = peers // 2
    scale = 1.0 / (peers * LANES)

    @pl.when(pl.program_id(0) == 0)
    def _():
        for k in range(1, slots):
            tw_ref[k] = jnp.broadcast_to(tab_ref[:, k : k + 1], (LANES, 128))
            tw_ref[slots + k] = jnp.broadcast_to(tab_ref[:, 64 + k : 65 + k], (LANES, 128))

    def spans(i):
        low = pl.multiple_of(i * 16, 16)
        return pl.ds(low, 16), pl.ds(pl.multiple_of(LANES + low, 16), 16)

    def before(i, carry):
        span, span_im = spans(i)
        bins = real_dft([z_ref[d, span, :].astype(F32) for d in range(peers)])
        y_ref[span, 0:128] = bins[0][0]
        y_ref[span_im, 0:128] = bins[slots][0]
        for k in range(1, slots):
            cos, sin = tw_ref[k, span, :], tw_ref[slots + k, span, :]
            re, im = bins[k]
            y_ref[span, 128 * k : 128 * k + 128] = re * cos + im * sin
            y_ref[span_im, 128 * k : 128 * k + 128] = re * sin - im * cos
        return carry

    lax.fori_loop(0, LANES // 16, before, 0)
    bound = bound_ref[...]

    def product(table, value):
        high, low = parts_of(value)
        return dot(table[0], high) + dot(table[0], low) + dot(table[1], high)

    row = lax.broadcasted_iota(jnp.int32, (COLS, 128), 0)
    inner = row & (LANES - 1)
    reach = jnp.where(inner < LANES // 2, peers * inner, peers // 2 + peers * (LANES - 1 - inner))
    reach = jnp.where(row == LANES, peers * (LANES // 2), reach)
    gain = jnp.where((row == 0) | (row == LANES), scale, 2.0 * scale)
    spec = product(pair_t_ref, y_ref[:, 0:128])
    spec = jnp.where(reach <= bound, spec * gain, 0.0)
    y_ref[:, 0:128] = product(pair_ref, spec)

    def filtered(first, width):
        at = pl.ds(pl.multiple_of(first * 128, 128), width)
        spec = product(full_ref, y_ref[:, at])
        inner = lax.broadcasted_iota(jnp.int32, (LANES, width), 0)
        lane = lax.broadcasted_iota(jnp.int32, (LANES, width), 1)
        k1 = first + lane // 128
        reach = jnp.where(inner < LANES // 2, k1 + peers * inner, peers * (LANES - inner) - k1)
        wide = bound if width == 128 else jnp.concatenate([bound] * (width // 128), axis=1)
        keep = reach <= wide
        spec = jnp.concatenate(
            [jnp.where(keep, spec[:LANES], 0.0), jnp.where(keep, -spec[LANES:], 0.0)], axis=0
        )
        y_ref[:, at] = product(full_ref, spec)

    def pairs(j, carry):
        filtered(1 + 2 * j, 256)
        return carry

    lax.fori_loop(0, slots // 2 - 1, pairs, 0)
    filtered(slots - 1, 128)

    def after(i, carry):
        span, span_im = spans(i)
        bins = [(y_ref[span, 0:128], None)]
        for k in range(1, slots):
            cos, sin = tw_ref[k, span, :] * scale, tw_ref[slots + k, span, :] * scale
            re, im = y_ref[span, 128 * k : 128 * k + 128], y_ref[span_im, 128 * k : 128 * k + 128]
            bins.append((re * cos - im * sin, re * sin + im * cos))
        bins.append((y_ref[span_im, 0:128], None))
        for d, value in enumerate(real_idft(bins)):
            out_ref[d, span, :] = value.astype(BF)
        return carry

    lax.fori_loop(0, LANES // 16, after, 0)


def channel_filter(z, bound, tab, full, pair, pair_t):
    peers, rows, width = z.shape
    const3 = lambda i: (0, 0, 0)
    return pl.pallas_call(
        channel_kernel,
        grid=(width // 128,),
        in_specs=[
            pl.BlockSpec((peers, rows, 128), lambda i: (0, 0, i)),
            pl.BlockSpec((1, 128), lambda i: (0, i)),
            pl.BlockSpec(tab.shape, lambda i: (0, 0)),
            pl.BlockSpec(full.shape, const3),
            pl.BlockSpec(pair.shape, const3),
            pl.BlockSpec(pair_t.shape, const3),
        ],
        out_specs=pl.BlockSpec((peers, rows, 128), lambda i: (0, 0, i)),
        out_shape=jax.ShapeDtypeStruct(z.shape, BF),
        scratch_shapes=[
            pltpu.VMEM((COLS, peers // 2 * 128), F32),
            pltpu.VMEM((peers, LANES, 128), F32),
        ],
        compiler_params=pltpu.CompilerParams(vmem_limit_bytes=56 << 20),
        name="channel_filter",
    )(z, bound, tab, full, pair, pair_t)


def inverse_kernel(*refs):
    chunks = refs[:-6]
    tw_ref, gain_ref, full_ref, pair_ref, out_ref, v_ref = refs[-6:]
    pieces, rows = chunks[0].shape[1], chunks[0].shape[2]
    scale = 1.0 / (RADIX * LANES)

    def product(first, slots, table, gain):
        value = jnp.concatenate(
            [
                chunk[pl.ds(first, slots), piece].reshape(slots * rows, 128)
                for chunk in chunks
                for piece in range(pieces)
            ],
            axis=1,
        )
        if gain is not None:
            value = (value.astype(F32) * gain).astype(BF)
        total = dot_t(value, table[0]) + dot_t(value, table[1])
        v_ref[pl.ds(first, slots)] = total.reshape(slots, rows, COLS)

    product(0, 1, pair_ref, gain_ref[...])

    def batch(g, carry):
        product(1 + 5 * g, 5, full_ref, None)
        return carry

    lax.fori_loop(0, 3, batch, 0)

    def group(i, carry):
        span = pl.ds(pl.multiple_of(i * 8, 8), 8)
        for half in range(2):
            at = slice(128 * half, 128 * half + 128)
            to = slice(LANES + 128 * half, LANES + 128 * half + 128)
            bins = [(v_ref[0, span, at], None)]
            for k in range(1, SLOTS):
                cos = tw_ref[k : k + 1, at] * scale
                sin = tw_ref[SLOTS + k : SLOTS + k + 1, at] * scale
                re, im = v_ref[k, span, at], v_ref[k, span, to]
                bins.append((re * cos - im * sin, re * sin + im * cos))
            bins.append((v_ref[0, span, to], None))
            for a, value in enumerate(real_idft(bins)):
                out_ref[span, LANES * a + 128 * half : LANES * a + 128 * half + 128] = value
        return carry

    lax.fori_loop(0, rows // 8, group, 0)


def inverse(chunks, tw, gain, full, pair):
    slots, pieces, rows, width = chunks[0].shape
    samples = RADIX * LANES
    tile = 64
    const2, const3 = lambda i: (0, 0), lambda i: (0, 0, 0)
    return pl.pallas_call(
        inverse_kernel,
        grid=(rows // tile,),
        in_specs=[pl.BlockSpec((slots, pieces, tile, width), lambda i: (0, 0, i, 0))] * len(chunks)
        + [
            pl.BlockSpec(tw.shape, const2),
            pl.BlockSpec(gain.shape, const2),
            pl.BlockSpec(full.shape, const3),
            pl.BlockSpec(pair.shape, const3),
        ],
        out_specs=pl.BlockSpec((tile, samples), lambda i: (i, 0)),
        out_shape=jax.ShapeDtypeStruct((rows, samples), F32),
        scratch_shapes=[pltpu.VMEM((SLOTS, tile, COLS), F32)],
        compiler_params=pltpu.CompilerParams(vmem_limit_bytes=56 << 20),
        name="time_inverse",
    )(*chunks, tw, gain, full, pair)


def detect_kernel(before_ref, mid_ref, after_ref, stack_ref, out_ref, sums_ref):
    rows, span = mid_ref.shape
    step = pl.program_id(0)
    block = 512
    tiles = rows // 32
    for b in range(span // block):
        at = slice(block * b, block * (b + 1))
        low = jnp.concatenate(
            [
                before_ref[:, at].astype(F32),
                mid_ref[:, at],
                after_ref[:, at].astype(F32),
                jnp.zeros((64, block), F32),
            ],
            axis=0,
        )
        turned = low.T.astype(BF)
        for j in range(tiles):
            base = j // 4 * 128
            shift = 96 - 32 * (j % 4)
            detection = dot(turned[:, base : base + 256], stack_ref[shift : shift + 256, :])
            squared = (detection * detection).reshape(block // WIN, WIN, 256)
            first = pl.multiple_of(step * (span // WIN) + b * (block // WIN), 8)
            sums_ref[pl.ds(first, 8), 256 * j : 256 * j + 256] = jnp.sum(squared, axis=1)

    @pl.when(step == pl.num_programs(0) - 1)
    def _():
        out_ref[...] = sums_ref[...].T * (1.0 / WIN)


def detect(before, filtered, after, stack, templates):
    rows, samples = filtered.shape
    span = 1024
    windows = samples // WIN
    return pl.pallas_call(
        detect_kernel,
        grid=(samples // span,),
        in_specs=[
            pl.BlockSpec((32, span), lambda i: (0, i)),
            pl.BlockSpec((rows, span), lambda i: (0, i)),
            pl.BlockSpec((32, span), lambda i: (0, i)),
            pl.BlockSpec(stack.shape, lambda i: (0, 0)),
        ],
        out_specs=pl.BlockSpec((rows * templates, windows), lambda i: (0, 0)),
        out_shape=jax.ShapeDtypeStruct((rows * templates, windows), F32),
        scratch_shapes=[pltpu.VMEM((windows, rows * templates), F32)],
        compiler_params=pltpu.CompilerParams(vmem_limit_bytes=56 << 20),
        name="detect",
    )(before, filtered, after, stack)


def plan(fan_bound, half):
    blocks = LANES // 2
    by_block = fan_bound.reshape(blocks, RADIX)
    cut = jnp.any((by_block >= 0) & (by_block < half), axis=1)
    position = lax.broadcasted_iota(jnp.int32, (blocks, blocks), 0)
    other = lax.broadcasted_iota(jnp.int32, (blocks, blocks), 1)
    ahead = jnp.where(cut[:, None] == cut[None, :], other < position, cut[None, :])
    rank = jnp.sum(ahead.astype(jnp.int32), axis=1)
    count = jnp.sum(cut.astype(jnp.int32))
    placed = rank[None, :, None] == lax.broadcasted_iota(jnp.int32, (blocks, blocks, 1), 0)
    moved = jnp.sum(jnp.where(placed, by_block[None, :, :], 0), axis=1).T
    mirror = jnp.concatenate([moved[SLOTS : SLOTS + 1], moved[:SLOTS:-1]], axis=0)
    rising, falling = (v.reshape(SLOTS, 4, blocks // 4) for v in (moved[:SLOTS], mirror))
    start = rank // 32 * 128 + rank % 32
    slot = lax.broadcasted_iota(jnp.int32, (SLOTS, 4, blocks // 4), 0)
    spot = lax.broadcasted_iota(jnp.int32, (SLOTS, 4, blocks // 4), 1) * 128 + lax.broadcasted_iota(
        jnp.int32, (SLOTS, 4, blocks // 4), 2
    )
    rising_im = jnp.where((slot == 0) & (spot == start[0]), -1, rising)
    bounds = jnp.concatenate([rising, rising_im, falling, falling], axis=2).reshape(SLOTS, COLS)
    dest = jnp.concatenate([start, start[::-1] + 64, start + 32, start[::-1] + 96])
    column = lax.broadcasted_iota(jnp.int32, (1, COLS), 1)
    single = (column == start[0]) | (column == start[0] + 32)
    return count, bounds, dest[:, None], single


def stacking(tap_offset, tap_weight):
    span = 2 * HALO + 1
    templates = tap_offset.shape[0]
    offsets_grid = jnp.arange(span, dtype=jnp.int32) - HALO
    matches = (tap_offset[:, :, None] == offsets_grid[None, None, :]).astype(F32)
    kernel_low = jnp.sum(tap_weight[:, :, None] * matches, axis=1).astype(BF)
    period = 257
    line = jnp.pad(kernel_low, ((0, 0), (1, period - 1 - span)))
    band = jnp.tile(line, (1, 32))[:, : 32 * 256].reshape(templates, 32, 256)
    band = jnp.transpose(band, (2, 1, 0)).reshape(256, 32 * templates)
    return jnp.pad(band, ((96, 0), (0, 0)))


def per_device(das_window, fan_bound, tap_offset, tap_weight):
    rows, samples = das_window.shape
    peers = lax.axis_size("chan")
    pieces = peers // SLOTS
    templates = tap_offset.shape[0]
    me = lax.axis_index("chan")
    full = jnp.asarray(split_table(full_table()))
    pair_np = split_table(paired_table())
    pair = jnp.asarray(pair_np)
    pair_t = jnp.asarray(np.ascontiguousarray(np.swapaxes(pair_np, 1, 2)))
    order = np.arange(SLOTS)[:, None] * np.arange(LANES)[None, :]
    angle = 2.0 * np.pi * order / samples
    tw = jnp.asarray(np.concatenate([np.cos(angle), np.sin(angle)]).astype(np.float32))
    tab_np = np.zeros((LANES, 128), np.float32)
    order = np.arange(LANES)[:, None] * np.arange(peers // 2)[None, :]
    angle = 2.0 * np.pi * order / (peers * LANES)
    tab_np[:, : peers // 2] = np.cos(angle)
    tab_np[:, 64 : 64 + peers // 2] = np.sin(angle)
    tab = jnp.asarray(tab_np)

    groups = COLS // 128 // pieces
    half = peers * LANES // 2
    count, bounds, dest, single = plan(fan_bound, half)
    needed = (count + 32 * pieces - 1) // (32 * pieces)
    column = lax.broadcasted_iota(jnp.int32, (SLOTS, COLS), 1)
    mask = ((column < needed * (128 * pieces)) | (bounds >= half)).astype(F32)[:, None, :]
    scale = 1.0 / samples
    gain = jnp.where(single, scale, 2.0 * scale).astype(F32)
    by_chunk = bounds.reshape(SLOTS, groups, pieces, 128).transpose(0, 2, 1, 3)
    bound = lax.dynamic_slice_in_dim(by_chunk.reshape(peers, groups, 128), me, 1, 0)[0]
    stack = stacking(tap_offset, tap_weight)

    made = forward(das_window, tw, dest, mask, full, pair, pieces)
    chunks, (full_moved, pair_moved) = made[:groups], made[groups:]
    chunks = [c.reshape(peers, rows, 128) for c in chunks]

    def exchange(n, values, limits):
        out = list(values)
        for g in range(n):
            there = lax.all_to_all(values[g], "chan", split_axis=0, concat_axis=0, tiled=True)
            wave = channel_filter(there, limits[g : g + 1], tab, full, pair, pair_t)
            out[g] = lax.all_to_all(wave, "chan", split_axis=0, concat_axis=0, tiled=True)
        return tuple(out)

    branches = [functools.partial(exchange, n) for n in range(groups + 1)]
    chunks = lax.switch(needed, branches, tuple(chunks), bound)
    chunks = [c.reshape(SLOTS, pieces, rows, 128) for c in chunks]
    filtered = inverse(chunks, tw, gain, full_moved, pair_moved)

    up = [(i, i + 1) for i in range(peers - 1)]
    down = [(i + 1, i) for i in range(peers - 1)]
    before = lax.ppermute(filtered[rows - 32 :].astype(BF), "chan", up)
    after = lax.ppermute(filtered[:32].astype(BF), "chan", down)
    energy = detect(before, filtered, after, stack, templates)
    return filtered, energy.reshape(rows, templates, samples // WIN)


def solution(mesh):
    return jax.shard_map(
        per_device,
        mesh=mesh,
        in_specs=(P(("survey", "chan"), None), P(), P(), P()),
        out_specs=(P(("survey", "chan"), None), P(("survey", "chan"), None, None)),
        check_vma=False,
    )
```

```python
import functools
import math

import jax
import jax.numpy as jnp
import ml_dtypes
import numpy as np
from jax import lax
from jax.experimental import pallas as pl
from jax.experimental.pallas import tpu as pltpu
from jax.sharding import PartitionSpec as P

HALO = 31
WIN = 64
RADIX = 32
LANES = 256
SLOTS = RADIX // 2
COLS = 2 * LANES
BF = jnp.bfloat16
F32 = jnp.float32


def split_table(table):
    high = table.astype(ml_dtypes.bfloat16)
    low = (table - high.astype(np.float64)).astype(ml_dtypes.bfloat16)
    return np.stack([high, low])


def full_table():
    index = np.arange(LANES)
    angle = 2.0 * np.pi * ((index[:, None] * index[None, :]) % LANES) / LANES
    cos, sin = np.cos(angle), np.sin(angle)
    return np.block([[cos, -sin], [sin, cos]])


def paired_table():
    half = LANES // 2
    sample = np.arange(LANES)[:, None]
    even = 2 * np.arange(half)[None, :]
    odd = 1 + 2 * np.arange(half)[None, ::-1]
    step = 2.0 * np.pi / (2 * LANES)
    even_angle, odd_angle = (sample * even) * step, (sample * odd) * step
    table = np.zeros((COLS, COLS))
    table[:LANES, :half] = np.cos(even_angle)
    table[:LANES, LANES : LANES + half] = -np.sin(even_angle)
    table[:LANES, LANES] = np.cos(np.pi * sample[:, 0])
    table[LANES:, half:LANES] = np.cos(odd_angle)
    table[LANES:, LANES + half :] = -np.sin(odd_angle)
    return table


def real_dft(values):
    count = len(values)
    if count == 2:
        return [(values[0] + values[1], None), (values[0] - values[1], None)]
    even, odd = real_dft(values[0::2]), real_dft(values[1::2])
    quarter = count // 4
    out = [None] * (count // 2 + 1)
    out[0] = (even[0][0] + odd[0][0], None)
    out[count // 2] = (even[0][0] - odd[0][0], None)
    out[quarter] = (even[quarter][0], -odd[quarter][0])
    for k in range(1, quarter):
        cos, sin = math.cos(2 * math.pi * k / count), math.sin(2 * math.pi * k / count)
        (er, ei), (dr, di) = even[k], odd[k]
        tr, ti = dr * cos + di * sin, di * cos - dr * sin
        out[k] = (er + tr, ei + ti)
        out[count // 2 - k] = (er - tr, ti - ei)
    return out


def real_idft(bins):
    count = 2 * (len(bins) - 1)
    if count == 2:
        return [bins[0][0] + bins[1][0], bins[0][0] - bins[1][0]]
    quarter = count // 4
    first, last = bins[0][0], bins[count // 2][0]
    even, odd = [(first + last, None)], [(first - last, None)]
    for k in range(1, quarter):
        cos, sin = math.cos(2 * math.pi * k / count), math.sin(2 * math.pi * k / count)
        (ar, ai), (br, bi) = bins[k], bins[count // 2 - k]
        even.append((ar + br, ai - bi))
        dr, di = ar - br, ai + bi
        odd.append((dr * cos - di * sin, dr * sin + di * cos))
    mr, mi = bins[quarter]
    even.append((2.0 * mr, None))
    odd.append((-2.0 * mi, None))
    out = [None] * count
    out[0::2] = real_idft(even)
    out[1::2] = real_idft(odd)
    return out


def parts_of(value):
    high = value.astype(BF)
    return high, (value - high.astype(F32)).astype(BF)


def dot(left, right):
    return jnp.dot(left, right, preferred_element_type=F32)


def dot_t(left, right):
    return lax.dot_general(left, right, (((1,), (1,)), ((), ())), preferred_element_type=F32)


def forward_kernel(x_ref, tw_ref, dest_ref, mask_ref, full_ref, pair_ref, *rest):
    groups = len(rest) - 3
    outs, (full_out, pair_out, y_ref) = rest[:groups], rest[groups:]
    rows = x_ref.shape[0]
    pieces = outs[0].shape[1]

    @pl.when(pl.program_id(0) == 0)
    def _():
        column = lax.broadcasted_iota(jnp.int32, (COLS, COLS), 1)
        moved = (column == dest_ref[...]).astype(F32).astype(BF)
        for level in range(2):
            full_out[level] = dot(full_ref[level], moved).astype(BF)
            pair_out[level] = dot(pair_ref[level], moved).astype(BF)

    def group(i, carry):
        span = pl.ds(pl.multiple_of(i * 8, 8), 8)
        for half in range(2):
            at = slice(128 * half, 128 * half + 128)
            to = slice(LANES + 128 * half, LANES + 128 * half + 128)
            values = [
                x_ref[span, LANES * a + 128 * half : LANES * a + 128 * half + 128]
                for a in range(RADIX)
            ]
            bins = real_dft(values)
            y_ref[0, span, at] = bins[0][0]
            y_ref[0, span, to] = bins[SLOTS][0]
            for k in range(1, SLOTS):
                cos, sin = tw_ref[k : k + 1, at], tw_ref[SLOTS + k : SLOTS + k + 1, at]
                re, im = bins[k]
                y_ref[k, span, at] = re * cos + im * sin
                y_ref[k, span, to] = im * cos - re * sin
        return carry

    lax.fori_loop(0, rows // 8, group, 0)

    def product(first, slots, table):
        high, low = parts_of(y_ref[pl.ds(first, slots)].reshape(slots * rows, COLS))
        value = dot(high, table[0]) + dot(low, table[0]) + dot(high, table[1])
        value = value.reshape(slots, rows, COLS) * mask_ref[pl.ds(first, slots)]
        value = value.astype(BF)
        for g in range(groups):
            for piece in range(pieces):
                lane = 128 * (g * pieces + piece)
                outs[g][pl.ds(first, slots), piece] = value[:, :, lane : lane + 128]

    product(0, 1, pair_out)

    def batch(g, carry):
        product(1 + 5 * g, 5, full_out)
        return carry

    lax.fori_loop(0, 3, batch, 0)


def forward(x, tw, dest, mask, full, pair, pieces):
    rows, samples = x.shape
    tile = 64
    groups = COLS // 128 // pieces
    const2, const3 = lambda i: (0, 0), lambda i: (0, 0, 0)
    chunk = jax.ShapeDtypeStruct((SLOTS, pieces, rows, 128), BF)
    table = jax.ShapeDtypeStruct(full.shape, BF)
    return pl.pallas_call(
        forward_kernel,
        grid=(rows // tile,),
        in_specs=[
            pl.BlockSpec((tile, samples), lambda i: (i, 0)),
            pl.BlockSpec(tw.shape, const2),
            pl.BlockSpec(dest.shape, const2),
            pl.BlockSpec(mask.shape, const3),
            pl.BlockSpec(full.shape, const3),
            pl.BlockSpec(pair.shape, const3),
        ],
        out_specs=[pl.BlockSpec((SLOTS, pieces, tile, 128), lambda i: (0, 0, i, 0))] * groups
        + [pl.BlockSpec(full.shape, const3)] * 2,
        out_shape=[chunk] * groups + [table] * 2,
        scratch_shapes=[pltpu.VMEM((SLOTS, tile, COLS), F32)],
        compiler_params=pltpu.CompilerParams(vmem_limit_bytes=56 << 20),
        name="time_forward",
    )(x, tw, dest, mask, full, pair)


def channel_kernel(z_ref, bound_ref, tab_ref, full_ref, pair_ref, pair_t_ref, out_ref, y_ref, tw_ref):
    peers = z_ref.shape[0]
    slots = peers // 2
    scale = 1.0 / (peers * LANES)

    @pl.when(pl.program_id(0) == 0)
    def _():
        def widen(i, carry):
            span = pl.ds(pl.multiple_of(i * 16, 16), 16)
            for k in range(1, slots):
                tw_ref[k, span, :] = jnp.broadcast_to(tab_ref[span, k : k + 1], (16, 128))
                tw_ref[slots + k, span, :] = jnp.broadcast_to(
                    tab_ref[span, 64 + k : 65 + k], (16, 128)
                )
            return carry

        lax.fori_loop(0, LANES // 16, widen, 0)

    def spans(i):
        low = pl.multiple_of(i * 16, 16)
        return pl.ds(low, 16), pl.ds(pl.multiple_of(LANES + low, 16), 16)

    def before(i, carry):
        span, span_im = spans(i)
        bins = real_dft([z_ref[d, span, :].astype(F32) for d in range(peers)])
        y_ref[span, 0:128] = bins[0][0]
        y_ref[span_im, 0:128] = bins[slots][0]
        for k in range(1, slots):
            cos, sin = tw_ref[k, span, :], tw_ref[slots + k, span, :]
            re, im = bins[k]
            y_ref[span, 128 * k : 128 * k + 128] = re * cos + im * sin
            y_ref[span_im, 128 * k : 128 * k + 128] = re * sin - im * cos
        return carry

    lax.fori_loop(0, LANES // 16, before, 0)
    bound = bound_ref[...]

    def product(table, value):
        high, low = parts_of(value)
        return dot(table[0], high) + dot(table[0], low) + dot(table[1], high)

    row = lax.broadcasted_iota(jnp.int32, (COLS, 128), 0)
    inner = row & (LANES - 1)
    reach = jnp.where(inner < LANES // 2, peers * inner, peers // 2 + peers * (LANES - 1 - inner))
    reach = jnp.where(row == LANES, peers * (LANES // 2), reach)
    gain = jnp.where((row == 0) | (row == LANES), scale, 2.0 * scale)
    spec = product(pair_t_ref, y_ref[:, 0:128])
    spec = jnp.where(reach <= bound, spec * gain, 0.0)
    y_ref[:, 0:128] = product(pair_ref, spec)

    def filtered(first, width):
        at = pl.ds(pl.multiple_of(first * 128, 128), width)
        spec = product(full_ref, y_ref[:, at])
        inner = lax.broadcasted_iota(jnp.int32, (LANES, width), 0)
        lane = lax.broadcasted_iota(jnp.int32, (LANES, width), 1)
        k1 = first + lane // 128
        reach = jnp.where(inner < LANES // 2, k1 + peers * inner, peers * (LANES - inner) - k1)
        wide = bound if width == 128 else jnp.concatenate([bound] * (width // 128), axis=1)
        keep = reach <= wide
        spec = jnp.concatenate(
            [jnp.where(keep, spec[:LANES], 0.0), jnp.where(keep, -spec[LANES:], 0.0)], axis=0
        )
        y_ref[:, at] = product(full_ref, spec)

    def single(k, carry):
        filtered(k, 128)
        return carry

    lax.fori_loop(1, slots, single, 0)

    def after(i, carry):
        span, span_im = spans(i)
        bins = [(y_ref[span, 0:128], None)]
        for k in range(1, slots):
            cos, sin = tw_ref[k, span, :] * scale, tw_ref[slots + k, span, :] * scale
            re, im = y_ref[span, 128 * k : 128 * k + 128], y_ref[span_im, 128 * k : 128 * k + 128]
            bins.append((re * cos - im * sin, re * sin + im * cos))
        bins.append((y_ref[span_im, 0:128], None))
        for d, value in enumerate(real_idft(bins)):
            out_ref[d, span, :] = value.astype(BF)
        return carry

    lax.fori_loop(0, LANES // 16, after, 0)


def channel_filter(z, bound, tab, full, pair, pair_t):
    peers, rows, width = z.shape
    const3 = lambda i: (0, 0, 0)
    return pl.pallas_call(
        channel_kernel,
        grid=(width // 128,),
        in_specs=[
            pl.BlockSpec((peers, rows, 128), lambda i: (0, 0, i)),
            pl.BlockSpec((1, 128), lambda i: (0, i)),
            pl.BlockSpec(tab.shape, lambda i: (0, 0)),
            pl.BlockSpec(full.shape, const3),
            pl.BlockSpec(pair.shape, const3),
            pl.BlockSpec(pair_t.shape, const3),
        ],
        out_specs=pl.BlockSpec((peers, rows, 128), lambda i: (0, 0, i)),
        out_shape=jax.ShapeDtypeStruct(z.shape, BF),
        scratch_shapes=[
            pltpu.VMEM((COLS, peers // 2 * 128), F32),
            pltpu.VMEM((peers, LANES, 128), F32),
        ],
        compiler_params=pltpu.CompilerParams(vmem_limit_bytes=56 << 20),
        name="channel_filter",
    )(z, bound, tab, full, pair, pair_t)


def inverse_kernel(groups, *refs):
    tw_ref, gain_ref, full_ref, pair_ref = refs[groups : groups + 4]
    chunks, v_ref = refs[:groups], refs[-1]
    edge = len(refs) == groups + 7 and refs[-2].dtype == BF
    out_ref = refs[-3] if edge else refs[-2]
    pieces, rows = chunks[0].shape[1], chunks[0].shape[2]
    scale = 1.0 / (RADIX * LANES)

    def product(first, slots, table, gain):
        value = jnp.concatenate(
            [
                chunk[pl.ds(first, slots), piece].reshape(slots * rows, 128)
                for chunk in chunks
                for piece in range(pieces)
            ],
            axis=1,
        )
        if gain is not None:
            value = (value.astype(F32) * gain).astype(BF)
        total = dot_t(value, table[0]) + dot_t(value, table[1])
        v_ref[pl.ds(first, slots)] = total.reshape(slots, rows, COLS)

    product(0, 1, pair_ref, gain_ref[...])

    def batch(g, carry):
        product(1 + 5 * g, 5, full_ref, None)
        return carry

    lax.fori_loop(0, 3, batch, 0)

    def group(i, carry):
        span = pl.ds(pl.multiple_of(i * 8, 8), 8)
        for half in range(2):
            at = slice(128 * half, 128 * half + 128)
            to = slice(LANES + 128 * half, LANES + 128 * half + 128)
            bins = [(v_ref[0, span, at], None)]
            for k in range(1, SLOTS):
                cos = tw_ref[k : k + 1, at] * scale
                sin = tw_ref[SLOTS + k : SLOTS + k + 1, at] * scale
                re, im = v_ref[k, span, at], v_ref[k, span, to]
                bins.append((re * cos - im * sin, re * sin + im * cos))
            bins.append((v_ref[0, span, to], None))
            for a, value in enumerate(real_idft(bins)):
                out_ref[span, LANES * a + 128 * half : LANES * a + 128 * half + 128] = value
        return carry

    lax.fori_loop(0, rows // 8, group, 0)
    if edge:
        first = pl.multiple_of(pl.program_id(0) * (rows - 32), 32)

        def rounded(i, carry):
            at = pl.ds(pl.multiple_of(i * 512, 512), 512)
            refs[-2][:, at] = out_ref[pl.ds(first, 32), at].astype(BF)
            return carry

        lax.fori_loop(0, out_ref.shape[1] // 512, rounded, 0)


def inverse(chunks, tw, gain, full, pair):
    slots, pieces, rows, width = chunks[0].shape
    samples = RADIX * LANES
    tile = 64
    tiles = rows // tile
    const2, const3 = lambda i: (0, 0), lambda i: (0, 0, 0)

    def call(steps, place, extra, more_specs, more_shapes, aliases):
        return pl.pallas_call(
            functools.partial(inverse_kernel, len(chunks)),
            grid=(steps,),
            in_specs=[pl.BlockSpec((slots, pieces, tile, width), lambda i: (0, 0, place(i), 0))]
            * len(chunks)
            + [
                pl.BlockSpec(tw.shape, const2),
                pl.BlockSpec(gain.shape, const2),
                pl.BlockSpec(full.shape, const3),
                pl.BlockSpec(pair.shape, const3),
            ]
            + [pl.BlockSpec(memory_space=pl.ANY)] * len(extra),
            out_specs=[pl.BlockSpec((tile, samples), lambda i: (place(i), 0))] + more_specs,
            out_shape=[jax.ShapeDtypeStruct((rows, samples), F32)] + more_shapes,
            scratch_shapes=[pltpu.VMEM((SLOTS, tile, COLS), F32)],
            input_output_aliases=aliases,
            compiler_params=pltpu.CompilerParams(vmem_limit_bytes=56 << 20),
            name="time_inverse",
        )(*chunks, tw, gain, full, pair, *extra)

    begun, edges = call(
        2,
        lambda i: i * (tiles - 1),
        (),
        [pl.BlockSpec((32, samples), lambda i: (i, 0))],
        [jax.ShapeDtypeStruct((64, samples), BF)],
        {},
    )
    (filtered,) = call(tiles - 2, lambda i: i + 1, (begun,), [], [], {len(chunks) + 4: 0})
    return filtered, edges


def detect_kernel(before_ref, mid_ref, after_ref, stack_ref, out_ref, sums_ref):
    rows, span = mid_ref.shape
    step = pl.program_id(0)
    block = 512
    tiles = rows // 32
    for b in range(span // block):
        at = slice(block * b, block * (b + 1))
        low = jnp.concatenate(
            [
                before_ref[:, at].astype(F32),
                mid_ref[:, at],
                after_ref[:, at].astype(F32),
                jnp.zeros((64, block), F32),
            ],
            axis=0,
        )
        turned = low.T.astype(BF)
        for j in range(tiles):
            base = j // 4 * 128
            shift = 96 - 32 * (j % 4)
            detection = dot(turned[:, base : base + 256], stack_ref[shift : shift + 256, :])
            squared = (detection * detection).reshape(block // WIN, WIN, 256)
            first = pl.multiple_of(step * (span // WIN) + b * (block // WIN), 8)
            sums_ref[pl.ds(first, 8), 256 * j : 256 * j + 256] = jnp.sum(squared, axis=1)

    @pl.when(step == pl.num_programs(0) - 1)
    def _():
        out_ref[...] = sums_ref[...].T * (1.0 / WIN)


def detect(before, filtered, after, stack, templates):
    rows, samples = filtered.shape
    span = 1024
    windows = samples // WIN
    return pl.pallas_call(
        detect_kernel,
        grid=(samples // span,),
        in_specs=[
            pl.BlockSpec((32, span), lambda i: (0, i)),
            pl.BlockSpec((rows, span), lambda i: (0, i)),
            pl.BlockSpec((32, span), lambda i: (0, i)),
            pl.BlockSpec(stack.shape, lambda i: (0, 0)),
        ],
        out_specs=pl.BlockSpec((rows * templates, windows), lambda i: (0, 0)),
        out_shape=jax.ShapeDtypeStruct((rows * templates, windows), F32),
        scratch_shapes=[pltpu.VMEM((windows, rows * templates), F32)],
        compiler_params=pltpu.CompilerParams(vmem_limit_bytes=56 << 20),
        name="detect",
    )(before, filtered, after, stack)


def plan(fan_bound, half):
    blocks = LANES // 2
    by_block = fan_bound.reshape(blocks, RADIX)
    cut = jnp.any((by_block >= 0) & (by_block < half), axis=1)
    position = lax.broadcasted_iota(jnp.int32, (blocks, blocks), 0)
    other = lax.broadcasted_iota(jnp.int32, (blocks, blocks), 1)
    ahead = jnp.where(cut[:, None] == cut[None, :], other < position, cut[None, :])
    rank = jnp.sum(ahead.astype(jnp.int32), axis=1)
    count = jnp.sum(cut.astype(jnp.int32))
    placed = rank[None, :, None] == lax.broadcasted_iota(jnp.int32, (blocks, blocks, 1), 0)
    moved = jnp.sum(jnp.where(placed, by_block[None, :, :], 0), axis=1).T
    mirror = jnp.concatenate([moved[SLOTS : SLOTS + 1], moved[:SLOTS:-1]], axis=0)
    rising, falling = (v.reshape(SLOTS, 4, blocks // 4) for v in (moved[:SLOTS], mirror))
    start = rank // 32 * 128 + rank % 32
    slot = lax.broadcasted_iota(jnp.int32, (SLOTS, 4, blocks // 4), 0)
    spot = lax.broadcasted_iota(jnp.int32, (SLOTS, 4, blocks // 4), 1) * 128 + lax.broadcasted_iota(
        jnp.int32, (SLOTS, 4, blocks // 4), 2
    )
    rising_im = jnp.where((slot == 0) & (spot == start[0]), -1, rising)
    bounds = jnp.concatenate([rising, rising_im, falling, falling], axis=2).reshape(SLOTS, COLS)
    dest = jnp.concatenate([start, start[::-1] + 64, start + 32, start[::-1] + 96])
    column = lax.broadcasted_iota(jnp.int32, (1, COLS), 1)
    single = (column == start[0]) | (column == start[0] + 32)
    return count, bounds, dest[:, None], single


def stacking(tap_offset, tap_weight):
    span = 2 * HALO + 1
    templates = tap_offset.shape[0]
    offsets_grid = jnp.arange(span, dtype=jnp.int32) - HALO
    matches = (tap_offset[:, :, None] == offsets_grid[None, None, :]).astype(F32)
    kernel_low = jnp.sum(tap_weight[:, :, None] * matches, axis=1).astype(BF)
    period = 257
    line = jnp.pad(kernel_low, ((0, 0), (1, period - 1 - span)))
    band = jnp.tile(line, (1, 32))[:, : 32 * 256].reshape(templates, 32, 256)
    band = jnp.transpose(band, (2, 1, 0)).reshape(256, 32 * templates)
    return jnp.pad(band, ((96, 0), (0, 0)))


def per_device(das_window, fan_bound, tap_offset, tap_weight):
    rows, samples = das_window.shape
    peers = lax.axis_size("chan")
    pieces = peers // SLOTS
    templates = tap_offset.shape[0]
    me = lax.axis_index("chan")
    full = jnp.asarray(split_table(full_table()))
    pair_np = split_table(paired_table())
    pair = jnp.asarray(pair_np)
    pair_t = jnp.asarray(np.ascontiguousarray(np.swapaxes(pair_np, 1, 2)))
    order = np.arange(SLOTS)[:, None] * np.arange(LANES)[None, :]
    angle = 2.0 * np.pi * order / samples
    tw = jnp.asarray(np.concatenate([np.cos(angle), np.sin(angle)]).astype(np.float32))
    tab_np = np.zeros((LANES, 128), np.float32)
    order = np.arange(LANES)[:, None] * np.arange(peers // 2)[None, :]
    angle = 2.0 * np.pi * order / (peers * LANES)
    tab_np[:, : peers // 2] = np.cos(angle)
    tab_np[:, 64 : 64 + peers // 2] = np.sin(angle)
    tab = jnp.asarray(tab_np)

    groups = COLS // 128 // pieces
    half = peers * LANES // 2
    count, bounds, dest, single = plan(fan_bound, half)
    needed = (count + 32 * pieces - 1) // (32 * pieces)
    column = lax.broadcasted_iota(jnp.int32, (SLOTS, COLS), 1)
    mask = ((column < needed * (128 * pieces)) | (bounds >= half)).astype(F32)[:, None, :]
    scale = 1.0 / samples
    gain = jnp.where(single, scale, 2.0 * scale).astype(F32)
    by_chunk = bounds.reshape(SLOTS, groups, pieces, 128).transpose(0, 2, 1, 3)
    bound = lax.dynamic_slice_in_dim(by_chunk.reshape(peers, groups, 128), me, 1, 0)[0]
    stack = stacking(tap_offset, tap_weight)

    made = forward(das_window, tw, dest, mask, full, pair, pieces)
    chunks, (full_moved, pair_moved) = made[:groups], made[groups:]
    chunks = [c.reshape(peers, rows, 128) for c in chunks]

    def exchange(n, values, limits, tables):
        out = list(values)
        for g in range(n):
            there = lax.all_to_all(values[g], "chan", split_axis=0, concat_axis=0, tiled=True)
            wave = channel_filter(there, limits[g : g + 1], *tables)
            out[g] = lax.all_to_all(wave, "chan", split_axis=0, concat_axis=0, tiled=True)
        return tuple(out)

    tables = lax.optimization_barrier((tab, full, pair, pair_t))
    branches = [functools.partial(exchange, n) for n in range(groups + 1)]
    chunks = lax.switch(needed, branches, tuple(chunks), bound, tables)
    chunks = [c.reshape(SLOTS, pieces, rows, 128) for c in chunks]
    filtered, edges = inverse(chunks, tw, gain, full_moved, pair_moved)

    up = [(i, i + 1) for i in range(peers - 1)]
    down = [(i + 1, i) for i in range(peers - 1)]
    before = lax.ppermute(edges[32:], "chan", up)
    after = lax.ppermute(edges[:32], "chan", down)
    energy = detect(before, filtered, after, stack, templates)
    return filtered, energy.reshape(rows, templates, samples // WIN)


def solution(mesh):
    return jax.shard_map(
        per_device,
        mesh=mesh,
        in_specs=(P(("survey", "chan"), None), P(), P(), P()),
        out_specs=(P(("survey", "chan"), None), P(("survey", "chan"), None, None)),
        check_vma=False,
    )
```
